32 devices in a mesh: pair: 8 (over y, x, core), idx: 4 (over z).
Axes of the slice: x: 2, y: 2, z: 4, core: 2. Of those that a mesh axis runs over, the one named last changes fastest.
Arguments:
- g2: bfloat16 [512, 512, 2, 1, 512], P('pair', None, None, None, 'idx'), may hold values from -6 to 6
- core_ham: float32 [512, 512], replicated, may hold values from -0.25 to 0.25
- dipole: float32 [512, 512], replicated, may hold values from -0.125 to 0.125
- field: float32 [1], replicated, may hold values from 0.5 to 1.5
- rho: bfloat16 [2, 512, 512], replicated, may hold values from -6 to 6
- factors: bfloat16 [2048, 512, 512], P(None, 'pair', 'idx'), may hold values from -0.046875 to 0.046875
- damping: float32 [512], replicated, may hold values from 0.02 to 0.2
Outputs:
- g2_next: bfloat16 [512, 512, 2, 1, 512], P('pair', None, None, None, 'idx')
The draws below stay inside these ranges and needn't reach their ends.
All inputs are finite; a program needn't handle non-finite values.
Results may differ from the reference program's by a relative error of at most 0.0056.
Values may be sent and summed in bfloat16 or wider, within the bound.
A program may use at most 384 MiB of HBM per device.

```python
import math
import jax
import jax.numpy as jnp
from jax import lax

N = 512
Q = 2048
JS = 1


def block_scale(key, dims, shards, low, largest):
    gain = 1.0
    for axis_at, parts in shards:
        heights = jax.random.uniform(jax.random.fold_in(jax.random.fold_in(key, 6), axis_at), (parts,), jnp.float32, low / len(shards), largest / len(shards))
        gain = gain * jnp.repeat(jnp.exp(heights), dims[axis_at] // parts).reshape((-1,) + (1,) * (len(dims) - 1 - axis_at))
    return gain


def normal_values(rng, extent, deviation, most, split=(), kind=jnp.bfloat16):
    gain = block_scale(rng, extent, split, -0.22, 0.18) if split else 1.0
    drawn = jax.random.normal(rng, extent, jnp.float32) * deviation * gain
    return jnp.minimum(jnp.maximum(drawn, -most), most).astype(kind)


def setup_inputs(seed: int = 0) -> dict:
    key_list = jax.random.split(jax.random.key(seed), 8)
    g2 = normal_values(key_list[0], (N, N, 2, JS, N), 1.0, 6.0, ((0, 8), (4, 4)))
    core_ham = normal_values(key_list[1], (N, N), N ** -0.5, 0.25, (), jnp.float32)
    dipole = normal_values(key_list[2], (N, N), (4 * N) ** -0.5, 0.125, (), jnp.float32)
    field = jnp.clip(jax.random.uniform(key_list[3], (1,), jnp.float32, 0.5, 1.5), 0.5, 1.5)
    rho = normal_values(key_list[4], (2, N, N), 1.0, 6.0)
    factors = normal_values(key_list[5], (Q, N, N), (32 * N) ** -0.5, 0.046875, ((1, 8), (2, 4)))
    damping = jnp.clip(jnp.exp(jax.random.uniform(key_list[6], (N,), jnp.float32, math.log(0.02), math.log(0.2))), 0.02, 0.2)
    return {"g2": g2, "core_ham": core_ham, "dipole": dipole, "field": field, "rho": rho, "factors": factors, "damping": damping}


def combine(total_x, total_z, rho_part):
    real = total_z[:, 0, None, None] * rho_part[0][None] - total_z[:, 1, None, None] * rho_part[1][None]
    imag = total_z[:, 0, None, None] * rho_part[1][None] + total_z[:, 1, None, None] * rho_part[0][None]
    return total_x + jnp.stack([real, imag], axis=1)


def reference(g2, core_ham, dipole, field, rho, factors, damping):
    step_size = 1.0
    hamil = 0.5 * (core_ham + core_ham.T) + field[0] * (0.5 * (dipole + dipole.T))
    ham_b = hamil.astype(jnp.bfloat16)
    ham_f = ham_b.astype(jnp.float32)
    slab_ham = ham_f[:JS, :JS]
    term_i = jnp.dot(ham_b, g2.reshape(N, -1), preferred_element_type=jnp.float32).astype(jnp.bfloat16).reshape(g2.shape)
    lflat = factors.reshape(Q, N * N)
    xsum = jnp.dot(lflat, g2.reshape(N * N, -1), preferred_element_type=jnp.float32)
    zsum = lax.dot_general(lflat, rho.reshape(2, N * N), (((1,), (1,)), ((), ())), preferred_element_type=jnp.float32)
    slab_rho = rho[:, :JS, :].astype(jnp.float32)
    aux = combine(xsum.reshape(Q, 2, JS, N), zsum, slab_rho).astype(jnp.bfloat16)
    aux_flat = aux.reshape(Q, -1)
    blocks = 8
    size_b = N // blocks

    def one_block(start):
        start = start.astype(jnp.int32)
        group_g = lax.dynamic_slice_in_dim(g2, start, size_b, 0)
        group_i = lax.dynamic_slice_in_dim(term_i, start, size_b, 0)
        lmat = lax.dynamic_slice_in_dim(factors, start, size_b, 1).reshape(Q, -1)
        gam_rows = lax.dynamic_slice_in_dim(damping, start, size_b, 0)
        ham_cols = jnp.dot(group_g.reshape(-1, N), ham_b, preferred_element_type=jnp.float32).reshape(group_g.shape)
        factor_term = lax.dot_general(lmat, aux_flat, (((0,), (0,)), ((), ())), preferred_element_type=jnp.float32).reshape(group_g.shape)
        part_two = (factor_term - ham_cols).astype(jnp.bfloat16)
        values = group_g.astype(jnp.float32)
        term_k = jnp.einsum("km,imr->ikr", ham_f, values.reshape(size_b, N, -1)).reshape(group_g.shape)
        term_j = jnp.einsum("jm,ikcml->ikcjl", slab_ham, values)
        rate = group_i.astype(jnp.float32) + part_two.astype(jnp.float32) + term_j - term_k
        decay = gam_rows[:, None, None, None] + damping[None, :, None, None] + damping[:JS][None, None, :, None] + damping[None, None, None, :]
        real_next = values[:, :, 0] + step_size * rate[:, :, 1] - step_size * decay * values[:, :, 0]
        imag_next = values[:, :, 1] - step_size * rate[:, :, 0] - step_size * decay * values[:, :, 1]
        return jnp.stack([real_next, imag_next], axis=2).astype(jnp.bfloat16)

    starts = jnp.arange(blocks, dtype=jnp.int32) * size_b
    result = lax.map(one_block, starts)
    return result.reshape(g2.shape)
```

```python
import functools

import jax
import jax.numpy as jnp
from jax import lax
from jax.experimental import pallas as pl
from jax.experimental.pallas import tpu as pltpu
from jax.sharding import PartitionSpec as P


def finish_kernel(sign, ham_ref, base_ref, rows_ref, h00_ref, own_ref, other_ref, first_ref, two_ref, out_ref):
    tile = own_ref.shape[0]
    width, cols = own_ref.shape[1:]
    start = pl.program_id(0) * tile
    wide = jnp.concatenate([other_ref[t] for t in range(tile)], axis=-1)
    term_k = jnp.dot(ham_ref[...], wide, preferred_element_type=jnp.float32)
    for t in range(tile):
        own = own_ref[t].astype(jnp.float32)
        other = other_ref[t].astype(jnp.float32)
        first = first_ref[:, t].reshape(width, cols).astype(jnp.float32)
        two = two_ref[:, t].reshape(width, cols).astype(jnp.float32)
        rate = first + two + h00_ref[0] * other - term_k[:, t * cols : (t + 1) * cols]
        decay = rows_ref[start + t] + base_ref[...]
        out_ref[t] = (own + sign * rate - decay * own).astype(out_ref.dtype)


def finish(sign, ham_b, base, gam_rows, h00, own, other, first, two):
    rows, width, cols = own.shape
    tile = min(4, rows)
    whole = lambda a: pl.BlockSpec(a.shape, lambda i: (0,) * a.ndim)
    smem = pl.BlockSpec(memory_space=pltpu.SMEM)
    plane = pl.BlockSpec((tile, width, cols), lambda i: (i, 0, 0))
    blocks = lambda a: pl.BlockSpec((a.shape[0], tile) + a.shape[2:], lambda i: (0, i, 0, 0))
    return pl.pallas_call(
        functools.partial(finish_kernel, sign),
        grid=(rows // tile,),
        in_specs=[whole(ham_b), whole(base), smem, smem, plane, plane, blocks(first), blocks(two)],
        out_specs=plane,
        out_shape=jax.ShapeDtypeStruct(own.shape, jnp.bfloat16),
        cost_estimate=pl.CostEstimate(
            flops=2 * own.size * width, bytes_accessed=10 * own.size, transcendentals=0
        ),
        compiler_params=pltpu.CompilerParams(vmem_limit_bytes=40 * 2**20),
    )(ham_b, base, gam_rows, h00, own, other, first, two)


def per_device(npair, nidx, g2, core_ham, dipole, field, rho, factors, damping):
    rows, width, _, slab, cols = g2.shape
    rank, _, kcols = factors.shape
    kpair = width // npair
    pair_pos = lax.axis_index("pair")
    idx_pos = lax.axis_index("idx")
    f32, bf16 = jnp.float32, jnp.bfloat16

    planes = [g2[:, :, c, 0, :] for c in range(2)]
    blocked = [
        jnp.swapaxes(x.reshape(rows, nidx, kcols, cols), 0, 1) for x in planes
    ]
    hamil = 0.5 * (core_ham + core_ham.T) + field[0] * (0.5 * (dipole + dipole.T))
    ham_b = hamil.astype(bf16)

    def exchange(x):
        got = lax.dynamic_update_slice_in_dim(
            jnp.zeros_like(x), lax.dynamic_slice_in_dim(x, idx_pos, 1, 0), idx_pos, 0
        )
        for d in range(1, nidx):
            ring = [(z, (z + d) % nidx) for z in range(nidx)]
            piece = lax.dynamic_slice_in_dim(x, lax.rem(idx_pos + d, nidx), 1, 0)
            piece = lax.ppermute(piece, "idx", ring)
            source = lax.rem(idx_pos + nidx - d, nidx)
            got = lax.dynamic_update_slice_in_dim(got, piece, source, 0)
        return got

    def spread(x):
        got = exchange(x)
        return jnp.moveaxis(got, 0, 2).reshape(rows, kcols, width)

    wide0 = spread(blocked[0])
    wide0, later = lax.optimization_barrier((wide0, blocked[1]))
    wide1 = spread(later)

    def first_index(x):
        send = jnp.swapaxes(x.reshape(rows, npair, kpair, cols), 0, 1)
        part = lax.all_to_all(send, "pair", split_axis=0, concat_axis=0)
        mixed = jnp.dot(ham_b, part.reshape(width, -1), preferred_element_type=f32)
        mixed = mixed.astype(bf16).reshape(npair, rows, kpair, cols)
        return lax.all_to_all(mixed, "pair", split_axis=0, concat_axis=0)

    firsts = [first_index(x) for x in planes]

    rho_rows = lax.dynamic_slice_in_dim(rho, pair_pos * rows, rows, 1)
    rho_local = lax.dynamic_slice_in_dim(rho_rows, idx_pos * kcols, kcols, 2)
    part_z = lax.dot_general(
        rho_local, factors, (((1, 2), (1, 2)), ((), ())), preferred_element_type=f32
    )
    zrows = part_z.reshape(-1, width)
    turned = jnp.swapaxes(factors, 0, 1)
    turned = lax.optimization_barrier(turned)

    def project(wide):
        return lax.dot_general(
            factors, wide, (((1, 2), (0, 1)), ((), ())), preferred_element_type=f32
        )

    rho0 = rho[:, 0, :].astype(f32)

    def back(wide, aux):
        ham_cols = jnp.dot(wide.reshape(-1, width), ham_b, preferred_element_type=f32)
        term = lax.dot_general(
            turned, aux, (((1,), (0,)), ((), ())), preferred_element_type=f32
        ).reshape(-1, width)
        two = (term - ham_cols).astype(bf16).reshape(rows, kcols, nidx, cols)
        return exchange(jnp.moveaxis(two, 2, 0))

    total0 = lax.psum(jnp.concatenate([project(wide0), zrows], axis=0), ("pair", "idx"))
    total_z = total0[rank:].reshape(2, rank)
    zre, zim = total_z[0][:, None], total_z[1][:, None]
    aux0 = (total0[:rank] + (zre * rho0[0][None] - zim * rho0[1][None])).astype(bf16)
    two0 = back(wide0, aux0)
    total1 = lax.psum(project(wide1) + 0.0 * total0[0, 0], ("pair", "idx"))
    aux1 = (total1 + (zre * rho0[1][None] + zim * rho0[0][None])).astype(bf16)
    two1 = back(wide1, aux1)

    gam_rows = lax.dynamic_slice_in_dim(damping, pair_pos * rows, rows, 0)
    gam_cols = lax.dynamic_slice_in_dim(damping, idx_pos * cols, cols, 0)
    base = damping[:, None] + damping[0] + gam_cols[None, :]
    h00 = ham_b[0, :1].astype(f32)
    args = (ham_b, base, gam_rows, h00)
    imag = finish(-1.0, *args, planes[1], planes[0], firsts[0], two0)
    real = finish(1.0, *args, planes[0], planes[1], firsts[1], two1)
    return jnp.stack([real, imag], axis=2)[:, :, :, None, :]


def solution(mesh):
    placed = (P("pair", None, None, None, "idx"), P(), P(), P(), P(), P(None, "pair", "idx"), P())
    return jax.shard_map(
        functools.partial(per_device, mesh.shape["pair"], mesh.shape["idx"]),
        mesh=mesh,
        in_specs=placed,
        out_specs=P("pair", None, None, None, "idx"),
        check_vma=False,
    )
```
